512 devices in a mesh: seq: 64 (over z, x), head: 8 (over y, core).
Axes of the slice: x: 4, y: 4, z: 16, core: 2. Of those that a mesh axis runs over, the one named last changes fastest.
Arguments:
- tokens: bfloat16 [8192, 4096], P('seq', 'head')
- gain: float32 [4096], replicated, may hold values from 0.25 to 1.75
- w_query: bfloat16 [4096, 2048], P('seq', 'head'), may hold values from -0.09375 to 0.09375
- w_key: bfloat16 [4096, 2048], P('seq', 'head'), may hold values from -0.09375 to 0.09375
- w_value: bfloat16 [4096, 2048], P('seq', 'head'), may hold values from -0.09375 to 0.09375
- w_out: bfloat16 [2048, 4096], P('head', 'seq'), may hold values from -0.125 to 0.125
- mem_query: bfloat16 [128, 2048], P(None, 'head'), may hold values from -12 to 12
- score_scale: float32 [16], P('head'), may hold values from 1.5 to 4
- decay: float32 [64, 16], P('seq', 'head'), may hold values from 0 to 1, as said below
- seg_len: int32 [64], P('seq'), may hold values from 32 to 128, as said below
Outputs:
- branch: bfloat16 [8192, 4096], P('seq', 'head')
The draws below stay inside these ranges and needn't reach their ends.
Inputs may be any that keep to these rules, and one draw needn't show every extreme that they name: `decay`: retention lies strictly between 0 and 1. `seg_len`: at least one segment is full and at least one holds exactly 32 valid tokens.
All inputs are finite; a program needn't handle non-finite values.
Results may differ from the reference program's by a relative error of at most 0.015.
Values may be sent and summed in bfloat16 or wider, within the bound.
A program may use at most 64 MiB of HBM per device.

```python
import math
import jax
import jax.numpy as jnp
from jax import lax

D = 4096
HEADS = 16
DH = 128
MEMORY_ROWS = 128
SEG = 128
LOG_PART_TOTAL = 64
TOKENS = 8192
HD = 2048
N_HEAD = 8


def draw_tokens(key, part):
    key_base, key_rows, key_cols = jax.random.split(key, 3)
    row_scale = jnp.exp(jax.random.uniform(key_rows, (TOKENS, 1), jnp.float32) * math.log(10.0))
    ramp = 1.0 + 2.0 * jnp.arange(D, dtype=jnp.float32)[None, :] / D
    col_scale = jnp.exp(jax.random.uniform(key_cols, (1, D), jnp.float32) * math.log(10.0)) * ramp
    base = jax.random.normal(key_base, (TOKENS, D), jnp.float32)
    return (base * row_scale * col_scale / 5.0).astype(jnp.bfloat16)


def draw_decay(key, part):
    selection_seed_stream, gradual_seed_stream, quick_seed_stream, multiplier_seed_stream, spike_seed_stream, threshold_seed_stream = jax.random.split(key, 6)
    share = 0.5
    gradual_sample = jax.random.uniform(selection_seed_stream, (HEADS,), jnp.float32) < share
    slow_rate = jnp.exp(jax.random.uniform(gradual_seed_stream, (HEADS,), jnp.float32, math.log(0.05), math.log(0.5))) / LOG_PART_TOTAL
    fast_rate = jnp.exp(jax.random.uniform(quick_seed_stream, (HEADS,), jnp.float32, math.log(1.5), math.log(4.0)))
    rate = jnp.where(gradual_sample, slow_rate, fast_rate)
    factor = jnp.exp(jax.random.uniform(multiplier_seed_stream, (LOG_PART_TOTAL, HEADS), jnp.float32, math.log(0.5), math.log(2.0)))
    selected_places = jax.random.randint(spike_seed_stream, (2,), 0, LOG_PART_TOTAL)
    spike_sample = jnp.zeros((LOG_PART_TOTAL,), jnp.float32).at[selected_places].set(1.0)
    cut = jax.random.uniform(threshold_seed_stream, (LOG_PART_TOTAL, HEADS), jnp.float32, 0.6, 0.8)
    match_indicator = (spike_sample[:, None] > 0.5) & gradual_sample[None, :]
    retain = jnp.exp(-rate[None, :] * factor) * jnp.where(match_indicator, cut, 1.0)
    return retain.astype(jnp.float32)


def draw_seg_len(key, part):
    key_len, key_first, key_second = jax.random.split(key, 3)
    lens = jax.random.randint(key_len, (LOG_PART_TOTAL,), SEG // 4, SEG + 1)
    first = jax.random.randint(key_first, (), 0, LOG_PART_TOTAL)
    second = (first + 1 + jax.random.randint(key_second, (), 0, LOG_PART_TOTAL - 1)) % LOG_PART_TOTAL
    lens = lens.at[first].set(SEG)
    lens = lens.at[second].set(SEG // 4)
    return lens.astype(jnp.int32)


def steps_of(stream_key, dims, shards, low, high):
    factor_of = 1.0
    for dim, blocks in shards:
        draws = jax.random.uniform(jax.random.fold_in(jax.random.fold_in(stream_key, 6), dim), (blocks,), jnp.float32, low / len(shards), high / len(shards))
        factor_of = factor_of * jnp.repeat(jnp.exp(draws), dims[dim] // blocks).reshape((-1,) + (1,) * (len(dims) - 1 - dim))
    return factor_of


def centred(own_key, dims, deviation, limit, cuts=(), held_as=jnp.bfloat16):
    values = deviation * jax.random.normal(own_key, dims, jnp.float32)
    if cuts:
        values = values * steps_of(own_key, dims, cuts, -0.22, 0.18)
    return jnp.clip(values, -limit, limit).astype(held_as)


def setup_inputs(seed: int = 0) -> dict:
    key_list = jax.random.split(jax.random.key(seed), 11)
    return {
        "tokens": draw_tokens(jax.random.fold_in(key_list[10], 71), 0),
        "gain": jnp.clip(1.0 + 0.15 * jax.random.normal(key_list[1], (D,), jnp.float32), 0.25, 1.75),
        "w_query": centred(key_list[2], (D, HD), D ** -0.5, 0.09375, ((0, 64), (1, 8))),
        "w_key": centred(key_list[3], (D, HD), D ** -0.5, 0.09375, ((0, 64), (1, 8))),
        "w_value": centred(key_list[4], (D, HD), D ** -0.5, 0.09375, ((0, 64), (1, 8))),
        "w_out": centred(key_list[5], (HD, D), HD ** -0.5, 0.125, ((0, 8), (1, 64))),
        "mem_query": centred(key_list[6], (MEMORY_ROWS, HD), 2.5, 12.0, ((1, 8),)),
        "score_scale": jnp.clip(jnp.exp(math.log(4.0) - 0.98082925 * jax.random.uniform(key_list[7], (HEADS,), jnp.float32) ** steps_of(key_list[7], (HEADS,), ((0, 8),), -0.2, 0.2)), 1.5, 4.0),
        "decay": draw_decay(jax.random.fold_in(key_list[10], 71), 0),
        "seg_len": draw_seg_len(jax.random.fold_in(key_list[10], 71), 0),
    }


def unit_rows(field):
    return field * lax.rsqrt(lax.optimization_barrier(jnp.mean(jnp.square(field), axis=-1, keepdims=True)) + 1e-06)

def rounded(field):
    return lax.optimization_barrier(field.astype(jnp.bfloat16)).astype(jnp.float32)

def reference(tokens, gain, w_query, w_key, w_value, w_out, mem_query, score_scale, decay, seg_len):
    head_columns = HEADS * DH
    group_cols = head_columns // N_HEAD
    inverse_root_scale = 1.0 / math.sqrt(DH)
    score_bias = math.log(MEMORY_ROWS + SEG)
    positions = jnp.arange(SEG, dtype=jnp.int32)
    causal = (positions[None, :] <= positions[:, None]).astype(jnp.float32)
    memory_head_split = mem_query.astype(jnp.float32).reshape(MEMORY_ROWS, HEADS, DH)
    head_scale_factors = (score_scale * inverse_root_scale)[:, None, None]
    out_groups = w_out.astype(jnp.float32).reshape(N_HEAD, group_cols, D)

    def segment(memory, inputs):
        block, retain, valid_len = inputs
        wide = block.astype(jnp.float32)
        normed = (wide * lax.rsqrt(lax.optimization_barrier(jnp.mean(wide * wide, axis=1, keepdims=True)) + 1e-05) * gain).astype(jnp.bfloat16)
        query = jnp.dot(normed, w_query, preferred_element_type=jnp.float32).astype(jnp.bfloat16)
        keys = jnp.dot(normed, w_key, preferred_element_type=jnp.float32).astype(jnp.bfloat16)
        values = jnp.dot(normed, w_value, preferred_element_type=jnp.float32).astype(jnp.bfloat16)
        query_head_split = query.astype(jnp.float32).reshape(SEG, HEADS, DH)
        key_head_split = keys.astype(jnp.float32).reshape(SEG, HEADS, DH)
        value_head_split = values.astype(jnp.float32).reshape(SEG, HEADS, DH)
        valid_keys = (positions < valid_len).astype(jnp.float32)
        memory_write_scores = jnp.einsum('bia,sia->ibs', memory_head_split, key_head_split) * inverse_root_scale
        memory_write_weights = rounded(jax.nn.sigmoid(memory_write_scores - math.log(SEG)) * valid_keys[None, None, :])
        memory_written_keys = jnp.einsum('elz,zek->lek', memory_write_weights, key_head_split).reshape(MEMORY_ROWS, head_columns)
        memory_written_values = jnp.einsum('elz,zek->lek', memory_write_weights, value_head_split).reshape(MEMORY_ROWS, head_columns)
        written = jnp.stack([memory_written_keys, memory_written_values])
        memory_unit_rows = rounded(unit_rows(memory.reshape(2, MEMORY_ROWS, HEADS, DH)))
        memory_score_matrix = jnp.einsum('zul,rul->uzr', query_head_split, memory_unit_rows[0]) * head_scale_factors
        tok_scores = jnp.einsum('thd,shd->hts', query_head_split, key_head_split) * head_scale_factors
        allowed = causal * valid_keys[None, :]
        memory_attention_weights = rounded(jax.nn.sigmoid(memory_score_matrix - score_bias))
        token_attention_weights = rounded(jax.nn.sigmoid(tok_scores - score_bias) * allowed[None, :, :])
        attended_output = jnp.einsum('krf,fku->rku', memory_attention_weights, memory_unit_rows[1]) + jnp.einsum('ymo,oyl->myl', token_attention_weights, value_head_split)
        attended_output = rounded(attended_output * valid_keys[:, None, None]).reshape(SEG, N_HEAD, group_cols)
        partials = rounded(jnp.einsum('tgc,gcd->gtd', attended_output, out_groups))
        branch = lax.optimization_barrier(jnp.sum(partials, axis=0)).astype(jnp.bfloat16)
        new_memory = jnp.repeat(retain, DH)[None, None, :] * memory + written
        return (new_memory, branch)
    start = jnp.zeros((2, MEMORY_ROWS, head_columns), jnp.float32)
    segments_in = (tokens.reshape(LOG_PART_TOTAL, SEG, D), decay, seg_len.astype(jnp.int32))
    _, branches = lax.scan(segment, start, segments_in)
    return branches.reshape(LOG_PART_TOTAL * SEG, D)
```

```python
import functools
import math

import jax
import jax.numpy as jnp
from jax import lax
from jax.experimental import pallas as pl
from jax.experimental.pallas import tpu as pltpu
from jax.sharding import PartitionSpec as P

MESH = pl.DeviceIdType.MESH
NX = 4
NC = 2
SEG = 128
DH = 128
ROWS = 64
F32 = jnp.float32
BF16 = jnp.bfloat16


def kernel(
    nz, ny,
    tok, gain, wq, wk, wv, wo, mq, scale, decay, seglen,
    out,
    wqb, wkb, wvb, wob, mqb, tsend, tkb, tgb,
    skv, rkv, sq, rq, sside, rside,
    tb, rb, eb, me, satt, ratt, pp, pr, ps, sb, orx,
    ring_s, ring_r, loc_s, mq_s, mq_r, t1_s, t1_r, t2_s, t2_r, t3_s, t3_r,
    kv_s, kv_r, q_s, q_r, sd_s, sd_r, wx_s, wx_r, wf_s,
    p1_s, p1_r, p2_s, p2_r, at_s, at_r, pa_s, pa_r, pb_s, pb_r,
):
    seq = lax.axis_index("seq")
    head = lax.axis_index("head")
    z, x = lax.div(seq, NX), lax.rem(seq, NX)
    y, c = lax.div(head, NC), lax.rem(head, NC)
    other = 1 - c
    hx, px = lax.div(x, 2), lax.rem(x, 2)
    features = nz * NX * ROWS

    def dev(zz, xx, yy, cc):
        return {"seq": zz * NX + xx, "head": yy * NC + cc}

    def rc(src, dst, ssem, rsem, target):
        return pltpu.make_async_remote_copy(
            src_ref=src, dst_ref=dst, send_sem=ssem, recv_sem=rsem,
            device_id=target, device_id_type=MESH,
        )

    zr, zl = lax.rem(z + 1, nz), lax.rem(z + nz - 1, nz)
    xs = [lax.rem(x + i, NX) for i in range(NX)]
    ys = [lax.rem(y + i, ny) for i in range(ny)]

    barrier = pltpu.get_barrier_semaphore()
    near = [dev(zr, x, y, c), dev(zl, x, y, c), dev(z, x, y, other)]
    near += [dev(z, xx, y, cc) for xx in xs[1:] for cc in range(NC)]
    near += [dev(z, x, yy, c) for yy in ys[1:]]
    for d in near:
        pl.semaphore_signal(barrier, inc=1, device_id=d, device_id_type=MESH)
    pl.semaphore_wait(barrier, len(near))

    srcs = (wk, wv, wo, wq)

    def slot(a, b):
        if a == 2:
            return wob.at[b, x]
        return (wkb, wvb, None, wqb)[a].at[b]

    def ring(a, way, t):
        step = t - 1
        b = lax.rem(z + nz - step, nz) if way == 0 else lax.rem(z + step, nz)
        first = isinstance(t, int) and t == 1
        return rc(srcs[a] if first else slot(a, b), slot(a, b),
                  ring_s.at[a, way, t], ring_r.at[a, b], dev(zr if way == 0 else zl, x, y, c))

    half = nz // 2

    def long_way(a):
        return a % 2

    def ring_first(a):
        for way in (0, 1):
            ring(a, way, 1).start()

    def ring_mid(arrays, t):
        for a in arrays:
            for way in (0, 1):
                cp = ring(a, way, t)
                cp.wait_recv()
                cp.start()

    def ring_last(arrays):
        for a in arrays:
            for way in (0, 1):
                cp = ring(a, way, half)
                cp.wait_recv()
                if way == long_way(a):
                    cp.start()
        for a in arrays:
            ring(a, long_way(a), half + 1).wait_recv()

    def ring_drain(a):
        for way in (0, 1):
            for t in range(1, half + (1 if way == long_way(a) else 0)):
                ring(a, way, t).wait_send()

    for a in range(4):
        ring_first(a)

    own = [pltpu.make_async_copy(srcs[a], slot(a, z), loc_s.at[a]) for a in range(4)]
    for cp in own:
        cp.start()
    mqc = rc(mq, mqb.at[c], mq_s, mq_r, dev(z, x, y, other))
    mqc.start()

    for i in range(NX):
        tsend[i] = jnp.concatenate(
            [tok[:, 64 * i:64 * i + 64], tok[:, 256 + 64 * i:256 + 64 * i + 64]], axis=1
        )

    def columns(h):
        return pl.ds(pl.multiple_of(h * 128, 128), 128)

    def rows(i):
        return pl.ds(pl.multiple_of(i * 128, 128), 128)

    h_me = y * NC + c

    def t1(i):
        xx = xs[i]
        return rc(tsend.at[xx], tkb.at[rows(x), columns(h_me)], t1_s.at[xx], t1_r.at[x],
                  dev(z, xx, y, c))

    for i in range(1, NX):
        t1(i).start()
    t1_own = pltpu.make_async_copy(tsend.at[x], tkb.at[rows(x), columns(h_me)], loc_s.at[4])
    t1_own.start()

    mid = (0, 1, 2, 3)

    def mid_steps(lo, hi):
        def step(t, carry):
            ring_mid(mid, t)
            return carry
        lax.fori_loop(lo, hi, step, 0)

    cut = min(3, half)
    mid_steps(2, cut)
    t1_own.wait()
    for i in range(1, NX):
        xx = xs[i]
        rc(tsend.at[xx], tkb.at[rows(xx), columns(h_me)], t1_s.at[xx], t1_r.at[xx],
           dev(z, xx, y, c)).wait_recv()

    def t2(i, hh):
        return rc(tkb.at[:, columns(hh)], tkb.at[:, columns(hh)], t2_s.at[i],
                  t2_r.at[lax.div(hh, NC)], dev(z, x, ys[i], c))

    def t3(hh):
        yy = lax.div(hh, NC)
        return rc(tkb.at[:, columns(hh)], tkb.at[:, columns(hh)], t3_s.at[yy], t3_r.at[yy],
                  dev(z, x, y, other))

    for i in range(1, ny):
        t2(i, h_me).start()
    t3(h_me).start()
    cut2 = min(cut + 3, half)
    mid_steps(cut, cut2)
    for i in range(1, ny):
        hh = ys[i] * NC + c
        t2(i, hh).wait_recv()
        t3(hh).start()
    mid_steps(cut2, half)
    ring_last(mid)
    for cp in own:
        cp.wait()

    hz = nz // 2

    def wpart(col, p):
        return wob.at[pl.ds(p * hz, hz), col]

    xr, xm, xl = xs[1], xs[2], xs[3]

    def wx(way, p):
        return rc(wpart(x, p), wpart(x, p), wx_s.at[way, p], wx_r.at[x, p],
                  dev(z, xr if way == 0 else xl, y, c))

    for p in (0, 1):
        wx(0, p).start()
        wx(1, 1 - p).start()

    for i in range(ny):
        hh = ys[i] * NC + other
        rc(tkb.at[:, columns(hh)], tkb.at[:, columns(hh)], t3_s.at[ys[i]], t3_r.at[ys[i]],
           dev(z, x, y, other)).wait_recv()

    ga = gain[pl.ds(hx, ny * NC, stride=4), :]
    gb = gain[pl.ds(2 + hx, ny * NC, stride=4), :]
    even = jnp.concatenate([ga[:, :64], gb[:, :64]], axis=1)
    odd = jnp.concatenate([ga[:, 64:], gb[:, 64:]], axis=1)
    g = jnp.where(px == 0, even, odd)
    ones = jnp.ones((8, 128), BF16)
    ss = jnp.zeros((8, NX * SEG), F32)
    for h in range(ny * NC):
        t = tkb[:, h * 128:h * 128 + 128].astype(F32)
        ss = ss + lax.dot_general(ones, (t * t).astype(BF16), (((1,), (1,)), ((), ())),
                                  preferred_element_type=F32)
        tgb[:, h * 128:h * 128 + 128] = (t * g[h:h + 1, :]).astype(BF16)

    depth = nz * ROWS
    big = tgb[...]
    for a, buf in enumerate((wkb, wvb, wqb)):
        part = jnp.dot(big, buf[...].reshape(depth, 2 * DH), preferred_element_type=F32)
        part = part.astype(BF16)
        for i in range(2):
            for cc in range(NC):
                block = part[cc * 256:cc * 256 + 256, i * DH:i * DH + DH]
                if a < 2:
                    skv[i, cc, :, a * DH:a * DH + DH] = block
                else:
                    sq[i, cc] = block
    row_id = lax.broadcasted_iota(jnp.int32, (8, 256), 0)
    length = seglen[0].astype(F32)
    for i in range(2):
        facts = jnp.where(row_id == 0, decay[0, i], jnp.where(row_id == 1, scale[0, i], length))
        for cc in range(NC):
            sside[i, cc, 0:8] = ss[:, cc * 256:cc * 256 + 256]
            sside[i, cc, 8:16] = facts

    trio = ((sside, rside, sd_s, sd_r), (skv, rkv, kv_s, kv_r), (sq, rq, q_s, q_r))

    def reduce_copy(i, cc, n):
        xx = 2 * c + i
        target = dev(z, xx, y, cc)
        src, dst, ssem, rsem = trio[n]
        return rc(src.at[i, cc], dst.at[x], ssem.at[i, cc], rsem.at[x], target)

    def local_copy(i, cc, n):
        src, dst, ssem, rsem = trio[n]
        return pltpu.make_async_copy(src.at[i, cc], dst.at[x], rsem.at[x])

    for n in range(3):
        for i in range(2):
            for cc in range(NC):
                mine = jnp.logical_and(x == 2 * c + i, c == cc)

                @pl.when(jnp.logical_not(mine))
                def _():
                    reduce_copy(i, cc, n).start()

                @pl.when(mine)
                def _():
                    local_copy(i, cc, n).start()

    def reduce_wait(n, xx):
        target = dev(z, x, y, other)
        src, dst, ssem, rsem = trio[n]
        rc(src.at[0, 0], dst.at[xx], ssem.at[0, 0], rsem.at[xx], target).wait_recv()

    for n in range(2):
        for xx in range(NX):
            reduce_wait(n, xx)

    total = rside[0, 0:8]
    for xx in range(1, NX):
        total = total + rside[xx, 0:8]
    r8 = lax.rsqrt(total * (1.0 / features) + 1e-05)
    kv = rkv[0].astype(F32)
    for xx in range(1, NX):
        kv = kv + rkv[xx].astype(F32)

    rt, keys, values, lens, decays = [], [], [], [], []
    for j in range(2):
        wide = jnp.broadcast_to(r8[0:1, j * 128:j * 128 + 128], (128, 128)).T
        rt.append(wide)
        part = kv[j * 128:j * 128 + 128]
        keys.append((part[:, :DH] * wide).astype(BF16))
        values.append((part[:, DH:] * wide).astype(BF16))
        facts = rside[2 * c + j, 8:16]
        decays.append(facts[0:1, 0:128])
        lens.append(facts[2:3, 0:128])
    score_scale = rside[x, 8:16][1:2, 0:128]

    inverse_root = 1.0 / math.sqrt(DH)
    rc(mq, mqb.at[other], mq_s, mq_r, dev(z, x, y, other)).wait_recv()
    mq_own = mq[:, pl.ds(pl.multiple_of(px * 128, 128), 128)]
    mq_other = mqb[other][:, :].astype(F32)
    mq_other = jnp.where(px == 0, mq_other[:, :DH], mq_other[:, DH:]).astype(BF16)
    mqh = jnp.where(hx == c, mq_own.astype(F32), mq_other.astype(F32)).astype(BF16)

    lane = lax.broadcasted_iota(jnp.int32, (SEG, SEG), 1).astype(F32)
    sub = lax.broadcasted_iota(jnp.int32, (SEG, SEG), 0).astype(F32)
    nt = (((1,), (1,)), ((), ()))
    written = []
    for j in range(2):
        s = lax.dot_general(mqh, keys[j], nt, preferred_element_type=F32) * inverse_root
        w = jax.nn.sigmoid(s - math.log(SEG))
        w = jnp.where(lane < lens[j], w, 0.0).astype(BF16)
        written.append((
            jnp.dot(w, keys[j], preferred_element_type=F32),
            jnp.dot(w, values[j], preferred_element_type=F32),
        ))

    np_ = nz * NC
    per = 2 * SEG // np_
    both = decays[0] * decays[1]
    hi = both.astype(BF16).astype(F32)
    lo = both - hi
    first = lax.broadcasted_iota(jnp.int32, (8, 128), 0) == 0
    dpiece = jnp.where(first, jnp.broadcast_to(hi, (8, 128)), jnp.broadcast_to(lo, (8, 128)))
    for u in range(2):
        t = decays[1] * written[0][u] + written[1][u]
        t = t.reshape(np_ // 2, per, 128)
        d = jnp.broadcast_to(dpiece[None], (np_ // 2, 8, 128))
        tb[u * (np_ // 2):(u + 1) * (np_ // 2)] = jnp.concatenate([t, d], axis=1).astype(BF16)

    g_me = z * NC + c

    def p1(k):
        o = lax.rem(g_me + k, np_)
        return rc(tb.at[o], rb.at[g_me], p1_s.at[k], p1_r.at[g_me],
                  dev(lax.div(o, NC), x, y, lax.rem(o, NC)))

    def p2(k):
        o = lax.rem(g_me + k, np_)
        return rc(eb.at[o], me.at[g_me], p2_s.at[k], p2_r.at[g_me],
                  dev(lax.div(o, NC), x, y, lax.rem(o, NC)))

    def loop(lo_, hi_, f):
        def body(k, carry):
            f(k)
            return carry
        lax.fori_loop(lo_, hi_, body, 0)

    loop(1, np_, lambda k: p1(k).start())
    p1_own = pltpu.make_async_copy(tb.at[g_me], rb.at[g_me], loc_s.at[5])
    p1_own.start()

    def wrelay(way):
        col = xl if way == 0 else xr
        return rc(wpart(col, way), wpart(col, way), wf_s.at[way], wx_r.at[col, way],
                  dev(z, xr if way == 0 else xl, y, c))

    for way in (0, 1):
        cp = wrelay(way)
        cp.wait_recv()
        cp.start()

    for xx in range(NX):
        reduce_wait(2, xx)
    qs = rq[0].astype(F32)
    for xx in range(1, NX):
        qs = qs + rq[xx].astype(F32)
    bias = math.log(SEG + SEG)
    factor = score_scale * inverse_root
    queries, token_part = [], []
    for j in range(2):
        q = (qs[j * 128:j * 128 + 128] * rt[j]).astype(BF16)
        queries.append(q)
        s = lax.dot_general(q, keys[j], nt, preferred_element_type=F32) * factor
        w = jax.nn.sigmoid(s - bias)
        keep = jnp.logical_and(lane <= sub, lane < lens[j])
        w = jnp.where(keep, w, 0.0).astype(BF16)
        token_part.append(jnp.dot(w, values[j], preferred_element_type=F32))

    def p1_arrival(k):
        o = lax.rem(g_me + k, np_)
        rc(tb.at[o], rb.at[o], p1_s.at[k], p1_r.at[o], dev(z, x, y, other)).wait_recv()

    p1_own.wait()
    loop(1, np_, p1_arrival)
    state = jnp.zeros((per, 128), F32)
    for k in range(np_):
        eb[k] = state.astype(BF16)
        piece = rb[k].astype(F32)
        state = (piece[per:per + 1] + piece[per + 1:per + 2]) * state + piece[0:per]
    loop(1, np_, lambda k: p2(k).start())
    p2_own = pltpu.make_async_copy(eb.at[g_me], me.at[g_me], loc_s.at[6])
    p2_own.start()

    def p2_arrival(k):
        o = lax.rem(g_me + k, np_)
        rc(eb.at[o], me.at[o], p2_s.at[k], p2_r.at[o], dev(z, x, y, other)).wait_recv()

    p2_own.wait()
    loop(1, np_, p2_arrival)
    entry = me[...].astype(F32).reshape(2, SEG, DH)

    def unit(m):
        return (m * lax.rsqrt(jnp.mean(m * m, axis=1, keepdims=True) + 1e-06)).astype(BF16)

    for j in range(2):
        if j == 0:
            mem = (entry[0], entry[1])
        else:
            mem = tuple(decays[0] * entry[u] + written[0][u] for u in range(2))
        mk, mv = unit(mem[0]), unit(mem[1])
        s = lax.dot_general(queries[j], mk, nt, preferred_element_type=F32) * factor
        w = jax.nn.sigmoid(s - bias).astype(BF16)
        a = jnp.dot(w, mv, preferred_element_type=F32) + token_part[j]
        satt[j] = jnp.where(sub < lens[j], a, 0.0).astype(BF16)

    def att_copy(j):
        return rc(satt.at[j], ratt.at[:, columns(px)], at_s.at[j], at_r.at[px],
                  dev(z, 2 * c + j, y, hx))

    for j in range(2):
        mine = jnp.logical_and(x == 2 * c + j, c == hx)

        @pl.when(jnp.logical_not(mine))
        def _():
            att_copy(j).start()

        @pl.when(mine)
        def _():
            pltpu.make_async_copy(satt.at[j], ratt.at[:, columns(px)], at_r.at[px]).start()

    for p in (0, 1):
        for col, done in ((xl, 0), (xr, 1)):
            if p != done:
                rc(wpart(col, p), wpart(col, p), wf_s.at[0], wx_r.at[col, p],
                   dev(z, xr, y, c)).wait_recv()
        rc(wpart(xm, p), wpart(xm, p), wf_s.at[0], wx_r.at[xm, p], dev(z, xr, y, c)).wait_recv()

    for j in range(2):
        rc(satt.at[j], ratt.at[:, j * 128:j * 128 + 128], at_s.at[j], at_r.at[j],
           dev(z, x, y, other)).wait_recv()

    att = ratt[...]
    nzs = nz // (ny * NC)

    def wblock(h):
        w = wob[pl.ds(h * nzs, nzs)]
        return w.reshape(nzs * NX * ROWS, 2 * DH)

    def pa(yy):
        return rc(pp.at[yy], pr.at[yy], pa_s.at[yy], pa_r.at[yy], dev(z, x, y, other))

    for yy in range(ny):
        pp[yy] = lax.dot_general(att, wblock(yy * NC + other), nt,
                                 preferred_element_type=F32).astype(BF16)
        pa(yy).start()
    for yy in range(ny):
        ps[yy] = lax.dot_general(att, wblock(yy * NC + c), nt, preferred_element_type=F32)

    def pb(i):
        return rc(sb.at[ys[i]], orx.at[y], pb_s.at[ys[i]], pb_r.at[y], dev(z, x, ys[i], c))

    for yy in range(ny):
        pa(yy).wait_recv()
    for i in list(range(1, ny)):
        sb[ys[i]] = (ps[ys[i]] + pr[ys[i]].astype(F32)).astype(BF16)
        pb(i).start()
    result = ps[y] + pr[y].astype(F32)
    for i in range(1, ny):
        rc(sb.at[ys[i]], orx.at[ys[i]], pb_s.at[ys[i]], pb_r.at[ys[i]],
           dev(z, x, ys[i], c)).wait_recv()
        result = result + orx[ys[i]].astype(F32)
    out[...] = result.astype(BF16)

    for a in range(4):
        ring_drain(a)
    mqc.wait_send()
    for i in range(1, NX):
        t1(i).wait_send()
    for i in range(1, ny):
        t2(i, h_me).wait_send()
    for i in range(ny):
        t3(ys[i] * NC + c).wait_send()
    for way in (0, 1):
        for p in (0, 1):
            wx(way, p).wait_send()
        wrelay(way).wait_send()
    for i in range(2):
        for cc in range(NC):
            mine = jnp.logical_and(x == 2 * c + i, c == cc)

            @pl.when(jnp.logical_not(mine))
            def _():
                for n in range(3):
                    reduce_copy(i, cc, n).wait_send()
    loop(1, np_, lambda k: p1(k).wait_send())
    loop(1, np_, lambda k: p2(k).wait_send())
    for j in range(2):
        mine = jnp.logical_and(x == 2 * c + j, c == hx)

        @pl.when(jnp.logical_not(mine))
        def _():
            att_copy(j).wait_send()
    for yy in range(ny):
        pa(yy).wait_send()
    for i in range(1, ny):
        pb(i).wait_send()


def solution(mesh):
    nz = mesh.shape["seq"] // NX
    ny = mesh.shape["head"] // NC

    def body(tokens, gain, w_query, w_key, w_value, w_out, mem_query, score_scale, decay, seg_len):
        vm = pl.BlockSpec(memory_space=pltpu.VMEM)
        sm = pl.BlockSpec(memory_space=pltpu.SMEM)
        np_ = nz * NC
        per = 2 * SEG // np_
        dma = pltpu.SemaphoreType.DMA
        width = tokens.shape[1]
        scratch = [
            pltpu.VMEM((nz, ROWS, 256), BF16),
            pltpu.VMEM((nz, ROWS, 256), BF16),
            pltpu.VMEM((nz, ROWS, 256), BF16),
            pltpu.VMEM((nz, NX, ROWS, 256), BF16),
            pltpu.VMEM((2, 128, 256), BF16),
            pltpu.VMEM((NX, 128, 128), BF16),
            pltpu.VMEM((NX * SEG, nz * ROWS), BF16),
            pltpu.VMEM((NX * SEG, nz * ROWS), BF16),
            pltpu.VMEM((2, NC, 256, 256), BF16),
            pltpu.VMEM((NX, 256, 256), BF16),
            pltpu.VMEM((2, NC, 256, 128), BF16),
            pltpu.VMEM((NX, 256, 128), BF16),
            pltpu.VMEM((2, NC, 16, 256), F32),
            pltpu.VMEM((NX, 16, 256), F32),
            pltpu.VMEM((np_, per + 8, 128), BF16),
            pltpu.VMEM((np_, per + 8, 128), BF16),
            pltpu.VMEM((np_, per, 128), BF16),
            pltpu.VMEM((np_, per, 128), BF16),
            pltpu.VMEM((2, 128, 128), BF16),
            pltpu.VMEM((128, 256), BF16),
            pltpu.VMEM((ny, 128, width), BF16),
            pltpu.VMEM((ny, 128, width), BF16),
            pltpu.VMEM((ny, 128, width), F32),
            pltpu.VMEM((ny, 128, width), BF16),
            pltpu.VMEM((ny, 128, width), BF16),
            dma((4, 2, nz // 2 + 2)), dma((4, nz)), dma((8,)), dma, dma,
            dma((NX,)), dma((NX,)), dma((ny,)), dma((ny,)), dma((ny,)), dma((ny,)),
            dma((2, 2)), dma((NX,)), dma((2, 2)), dma((NX,)), dma((2, 2)), dma((NX,)),
            dma((2, 2)), dma((NX, 2)), dma((2,)),
            dma((np_,)), dma((np_,)), dma((np_,)), dma((np_,)),
            dma((2,)), dma((2,)), dma((ny,)), dma((ny,)), dma((ny,)), dma((ny,)),
        ]
        return pl.pallas_call(
            functools.partial(kernel, nz, ny),
            out_shape=jax.ShapeDtypeStruct(tokens.shape, BF16),
            in_specs=[vm] * 7 + [sm] * 3,
            out_specs=vm,
            scratch_shapes=scratch,
            compiler_params=pltpu.CompilerParams(
                collective_id=0, has_side_effects=True, vmem_limit_bytes=48 * 1024 * 1024
            ),
        )(
            tokens, gain.reshape(-1, 128), w_query, w_key, w_value, w_out.T, mem_query,
            score_scale.reshape(1, 2), decay, seg_len,
        )

    return jax.shard_map(
        body,
        mesh=mesh,
        in_specs=(
            P("seq", "head"), P(None), P("seq", "head"), P("seq", "head"), P("seq", "head"),
            P("head", "seq"), P(None, "head"), P("head"), P("seq", "head"), P("seq"),
        ),
        out_specs=P("seq", "head"),
        check_vma=False,
    )
```

```python
import functools
import math

import jax
import jax.numpy as jnp
from jax import lax
from jax.experimental import pallas as pl
from jax.experimental.pallas import tpu as pltpu
from jax.sharding import PartitionSpec as P

MESH = pl.DeviceIdType.MESH
NX = 4
NC = 2
SEG = 128
DH = 128
ROWS = 64
F32 = jnp.float32
BF16 = jnp.bfloat16


def kernel(
    nz, ny,
    tok_h, gain_h, wq, wk, wv, wo, mq_h, scale_h, decay_h, seglen_h,
    out,
    tok, gain, mq, scale, decay, seglen,
    wqb, wkb, wvb, wr, ws, wf, mqb, tsend, tkb, tgb,
    skv, rkv, sq, rq, sside, rside,
    tb, rb, eb, me, satt, ratt, sb, orx,
    ring_s, ring_r, loc_s, mq_s, mq_r, t1_s, t1_r, t2_s, t2_r, t3_s, t3_r,
    kv_s, kv_r, q_s, q_r, sd_s, sd_r, sw_s, sw_r, wx_s, wx_r, wf_s,
    p1_s, p1_r, p2_s, p2_r, at_s, at_r, pb_s, pb_r, in_s,
):
    seq = lax.axis_index("seq")
    head = lax.axis_index("head")
    z, x = lax.div(seq, NX), lax.rem(seq, NX)
    y, c = lax.div(head, NC), lax.rem(head, NC)
    other = 1 - c
    hx, px = lax.div(x, 2), lax.rem(x, 2)
    features = nz * NX * ROWS

    def dev(zz, xx, yy, cc):
        return {"seq": zz * NX + xx, "head": yy * NC + cc}

    def rc(src, dst, ssem, rsem, target):
        return pltpu.make_async_remote_copy(
            src_ref=src, dst_ref=dst, send_sem=ssem, recv_sem=rsem,
            device_id=target, device_id_type=MESH,
        )

    zr, zl = lax.rem(z + 1, nz), lax.rem(z + nz - 1, nz)
    xs = [lax.rem(x + i, NX) for i in range(NX)]
    ys = [lax.rem(y + i, ny) for i in range(ny)]

    stage = [
        pltpu.make_async_copy(a, b, in_s.at[n])
        for n, (a, b) in enumerate((
            (tok_h, tok), (gain_h, gain), (mq_h, mq), (scale_h, scale), (decay_h, decay),
            (seglen_h, seglen),
        ))
    ]
    for cp in stage:
        cp.start()

    barrier = pltpu.get_barrier_semaphore()
    near = [dev(zr, x, y, c), dev(zl, x, y, c), dev(z, x, y, other)]
    near += [dev(z, xx, y, cc) for xx in xs[1:] for cc in range(NC)]
    near += [dev(z, x, yy, c) for yy in ys[1:]]
    for d in near:
        pl.semaphore_signal(barrier, inc=1, device_id=d, device_id_type=MESH)
    pl.semaphore_wait(barrier, len(near))

    srcs = (wk, wv, wo, wq)

    def slot(a, b):
        if a == 2:
            return wr.at[lax.div(b, 2 * NC), lax.rem(lax.div(b, 2), NC), lax.rem(b, 2)]
        return (wkb, wvb, None, wqb)[a].at[b]

    def ring(a, way, t):
        step = t - 1
        b = lax.rem(z + nz - step, nz) if way == 0 else lax.rem(z + step, nz)
        first = isinstance(t, int) and t == 1
        return rc(srcs[a] if first else slot(a, b), slot(a, b),
                  ring_s.at[a, way, t], ring_r.at[a, b], dev(zr if way == 0 else zl, x, y, c))

    half = nz // 2

    def long_way(a):
        return a % 2

    def ring_first(a):
        for way in (0, 1):
            ring(a, way, 1).start()

    def ring_mid(arrays, t):
        for a in arrays:
            for way in (0, 1):
                cp = ring(a, way, t)
                cp.wait_recv()
                cp.start()

    def ring_last(arrays):
        for a in arrays:
            for way in (0, 1):
                cp = ring(a, way, half)
                cp.wait_recv()
                if way == long_way(a):
                    cp.start()
        for a in arrays:
            ring(a, long_way(a), half + 1).wait_recv()

    def ring_drain(a):
        for way in (0, 1):
            for t in range(1, half + (1 if way == long_way(a) else 0)):
                ring(a, way, t).wait_send()

    early = (0, 1, 3, 2)
    for a in early:
        ring_first(a)

    own = [pltpu.make_async_copy(srcs[a], slot(a, z), loc_s.at[a]) for a in range(4)]
    for cp in own:
        cp.start()

    stage[0].wait()
    for i in range(NX):
        tsend[i] = jnp.concatenate(
            [tok[:, 64 * i:64 * i + 64], tok[:, 256 + 64 * i:256 + 64 * i + 64]], axis=1
        )

    def columns(h):
        return pl.ds(pl.multiple_of(h * 128, 128), 128)

    def rows(i):
        return pl.ds(pl.multiple_of(i * 128, 128), 128)

    h_me = y * NC + c

    def t1(i):
        xx = xs[i]
        return rc(tsend.at[xx], tkb.at[rows(x), columns(h_me)], t1_s.at[xx], t1_r.at[x],
                  dev(z, xx, y, c))

    for i in range(1, NX):
        t1(i).start()
    t1_own = pltpu.make_async_copy(tsend.at[x], tkb.at[rows(x), columns(h_me)], loc_s.at[4])
    t1_own.start()

    stage[2].wait()
    mqc = rc(mq, mqb.at[c], mq_s, mq_r, dev(z, x, y, other))
    mqc.start()

    steps = list(range(2, half)) + [half]

    def advance(n):
        for t in steps[:n]:
            if t < half:
                ring_mid(early, t)
            else:
                ring_last(early)
        del steps[:n]

    advance(1)
    t1_own.wait()
    for i in range(1, NX):
        xx = xs[i]
        rc(tsend.at[xx], tkb.at[rows(xx), columns(h_me)], t1_s.at[xx], t1_r.at[xx],
           dev(z, xx, y, c)).wait_recv()

    def t2(i, hh):
        return rc(tkb.at[:, columns(hh)], tkb.at[:, columns(hh)], t2_s.at[i],
                  t2_r.at[lax.div(hh, NC)], dev(z, x, ys[i], c))

    def t3(hh):
        yy = lax.div(hh, NC)
        return rc(tkb.at[:, columns(hh)], tkb.at[:, columns(hh)], t3_s.at[yy], t3_r.at[yy],
                  dev(z, x, y, other))

    for i in range(1, ny):
        t2(i, h_me).start()
    t3(h_me).start()
    advance(2)
    for i in range(1, ny):
        hh = ys[i] * NC + c
        t2(i, hh).wait_recv()
        t3(hh).start()
    stage[1].wait()
    ga = gain[pl.ds(hx, ny * NC, stride=4), :]
    gb = gain[pl.ds(2 + hx, ny * NC, stride=4), :]
    even = jnp.concatenate([ga[:, :64], gb[:, :64]], axis=1)
    odd = jnp.concatenate([ga[:, 64:], gb[:, 64:]], axis=1)
    g = jnp.where(px == 0, even, odd)
    ones = jnp.ones((8, 128), BF16)

    def stats(h, ss):
        t = tkb[:, h * 128:h * 128 + 128].astype(F32)
        tgb[:, h * 128:h * 128 + 128] = (t * g[h:h + 1, :]).astype(BF16)
        return ss + lax.dot_general(ones, (t * t).astype(BF16), (((1,), (1,)), ((), ())),
                                    preferred_element_type=F32)

    advance(2)
    for i in range(ny):
        hh = ys[i] * NC + other
        rc(tkb.at[:, columns(hh)], tkb.at[:, columns(hh)], t3_s.at[ys[i]], t3_r.at[ys[i]],
           dev(z, x, y, other)).wait_recv()
    ss = jnp.zeros((8, NX * SEG), F32)
    for h in range(ny):
        ss = stats(h, ss)
    advance(1)
    for h in range(ny, ny * NC):
        ss = stats(h, ss)
    advance(len(steps))
    for cp in own:
        cp.wait()

    wmine = wr.at[:, c]
    swap = rc(wr.at[:, other], ws, sw_s, sw_r, dev(z, x, y, other))
    swap.start()
    xr, xm, xl = xs[1], xs[2], xs[3]

    def wx(way, p):
        return rc(wmine if p == 0 else ws, wf.at[p, x], wx_s.at[way, p], wx_r.at[p, x],
                  dev(z, xr if way == 0 else xl, y, c))

    wx_own = [pltpu.make_async_copy(wmine if p == 0 else ws, wf.at[p, x], loc_s.at[7 + p])
              for p in (0, 1)]

    depth = nz * ROWS
    def project(a, buf):
        part = jnp.dot(tgb[...], buf[...].reshape(depth, 2 * DH), preferred_element_type=F32)
        part = part.astype(BF16)
        for i in range(2):
            for cc in range(NC):
                block = part[cc * 256:cc * 256 + 256, i * DH:i * DH + DH]
                if a < 2:
                    skv[i, cc, :, a * DH:a * DH + DH] = block
                else:
                    sq[i, cc] = block

    for cp in stage[3:]:
        cp.wait()
    row_id = lax.broadcasted_iota(jnp.int32, (8, 256), 0)
    length = seglen[0].astype(F32)
    for i in range(2):
        facts = jnp.where(row_id == 0, decay[0, i], jnp.where(row_id == 1, scale[0, i], length))
        for cc in range(NC):
            sside[i, cc, 0:8] = ss[:, cc * 256:cc * 256 + 256]
            sside[i, cc, 8:16] = facts

    trio = ((sside, rside, sd_s, sd_r), (skv, rkv, kv_s, kv_r), (sq, rq, q_s, q_r))

    def reduce_copy(i, cc, n):
        xx = 2 * c + i
        target = dev(z, xx, y, cc)
        src, dst, ssem, rsem = trio[n]
        return rc(src.at[i, cc], dst.at[x], ssem.at[i, cc], rsem.at[x], target)

    def local_copy(i, cc, n):
        src, dst, ssem, rsem = trio[n]
        return pltpu.make_async_copy(src.at[i, cc], dst.at[x], rsem.at[x])

    def reduce_start(n):
        for i in range(2):
            for cc in range(NC):
                mine = jnp.logical_and(x == 2 * c + i, c == cc)

                @pl.when(jnp.logical_not(mine))
                def _():
                    reduce_copy(i, cc, n).start()

                @pl.when(mine)
                def _():
                    local_copy(i, cc, n).start()

    reduce_start(0)
    project(0, wkb)
    project(1, wvb)
    reduce_start(1)
    project(2, wqb)
    reduce_start(2)

    def reduce_wait(n, xx):
        target = dev(z, x, y, other)
        src, dst, ssem, rsem = trio[n]
        rc(src.at[0, 0], dst.at[xx], ssem.at[0, 0], rsem.at[xx], target).wait_recv()

    for n in range(2):
        for xx in range(NX):
            reduce_wait(n, xx)
    for way in (0, 1):
        wx(way, 0).start()
    swap.wait_recv()
    for way in (0, 1):
        wx(way, 1).start()
    for cp in wx_own:
        cp.start()

    total = rside[0, 0:8]
    for xx in range(1, NX):
        total = total + rside[xx, 0:8]
    r8 = lax.rsqrt(total * (1.0 / features) + 1e-05)
    kv = rkv[0].astype(F32)
    for xx in range(1, NX):
        kv = kv + rkv[xx].astype(F32)

    rt, keys, values, lens, decays = [], [], [], [], []
    for j in range(2):
        wide = jnp.broadcast_to(r8[0:1, j * 128:j * 128 + 128], (128, 128)).T
        rt.append(wide)
        part = kv[j * 128:j * 128 + 128]
        keys.append((part[:, :DH] * wide).astype(BF16))
        values.append((part[:, DH:] * wide).astype(BF16))
        facts = rside[2 * c + j, 8:16]
        decays.append(facts[0:1, 0:128])
        lens.append(facts[2:3, 0:128])
    score_scale = rside[x, 8:16][1:2, 0:128]

    inverse_root = 1.0 / math.sqrt(DH)
    rc(mq, mqb.at[other], mq_s, mq_r, dev(z, x, y, other)).wait_recv()
    mq_own = mq[:, pl.ds(pl.multiple_of(px * 128, 128), 128)]
    mq_other = mqb[other][:, :].astype(F32)
    mq_other = jnp.where(px == 0, mq_other[:, :DH], mq_other[:, DH:]).astype(BF16)
    mqh = jnp.where(hx == c, mq_own.astype(F32), mq_other.astype(F32)).astype(BF16)

    lane = lax.broadcasted_iota(jnp.int32, (SEG, SEG), 1).astype(F32)
    sub = lax.broadcasted_iota(jnp.int32, (SEG, SEG), 0).astype(F32)
    nt = (((1,), (1,)), ((), ()))
    written = []
    for j in range(2):
        s = lax.dot_general(mqh, keys[j], nt, preferred_element_type=F32) * inverse_root
        w = jax.nn.sigmoid(s - math.log(SEG))
        w = jnp.where(lane < lens[j], w, 0.0).astype(BF16)
        written.append((
            jnp.dot(w, keys[j], preferred_element_type=F32),
            jnp.dot(w, values[j], preferred_element_type=F32),
        ))

    np_ = nz * NC
    per = 2 * SEG // np_
    both = decays[0] * decays[1]
    hi = both.astype(BF16).astype(F32)
    lo = both - hi
    first = lax.broadcasted_iota(jnp.int32, (8, 128), 0) == 0
    dpiece = jnp.where(first, jnp.broadcast_to(hi, (8, 128)), jnp.broadcast_to(lo, (8, 128)))
    for u in range(2):
        t = decays[1] * written[0][u] + written[1][u]
        t = t.reshape(np_ // 2, per, 128)
        d = jnp.broadcast_to(dpiece[None], (np_ // 2, 8, 128))
        tb[u * (np_ // 2):(u + 1) * (np_ // 2)] = jnp.concatenate([t, d], axis=1).astype(BF16)

    g_me = z * NC + c

    def p1(k):
        o = lax.rem(g_me + k, np_)
        return rc(tb.at[o], rb.at[g_me], p1_s.at[k], p1_r.at[g_me],
                  dev(lax.div(o, NC), x, y, lax.rem(o, NC)))

    def p2(k):
        o = lax.rem(g_me + k, np_)
        return rc(eb.at[o], me.at[g_me], p2_s.at[k], p2_r.at[g_me],
                  dev(lax.div(o, NC), x, y, lax.rem(o, NC)))

    def loop(lo_, hi_, f):
        def body(k, carry):
            f(k)
            return carry
        lax.fori_loop(lo_, hi_, body, 0)

    loop(1, np_, lambda k: p1(k).start())
    p1_own = pltpu.make_async_copy(tb.at[g_me], rb.at[g_me], loc_s.at[5])
    p1_own.start()

    def wrelay(way):
        col = xl if way == 0 else xr
        return rc(wf.at[way, col], wf.at[way, col], wf_s.at[way], wx_r.at[way, col],
                  dev(z, xr if way == 0 else xl, y, c))


    for xx in range(NX):
        reduce_wait(2, xx)
    qs = rq[0].astype(F32)
    for xx in range(1, NX):
        qs = qs + rq[xx].astype(F32)
    bias = math.log(SEG + SEG)
    factor = score_scale * inverse_root
    queries, token_part = [], []
    for j in range(2):
        q = (qs[j * 128:j * 128 + 128] * rt[j]).astype(BF16)
        queries.append(q)
        s = lax.dot_general(q, keys[j], nt, preferred_element_type=F32) * factor
        w = jax.nn.sigmoid(s - bias)
        keep = jnp.logical_and(lane <= sub, lane < lens[j])
        w = jnp.where(keep, w, 0.0).astype(BF16)
        token_part.append(jnp.dot(w, values[j], preferred_element_type=F32))

    wrelay(0).wait_recv()
    wrelay(0).start()

    def p1_arrival(k):
        o = lax.rem(g_me + k, np_)
        rc(tb.at[o], rb.at[o], p1_s.at[k], p1_r.at[o], dev(z, x, y, other)).wait_recv()

    p1_own.wait()
    loop(1, np_, p1_arrival)
    state = jnp.zeros((per, 128), F32)
    for k in range(np_):
        eb[k] = state.astype(BF16)
        piece = rb[k].astype(F32)
        state = (piece[per:per + 1] + piece[per + 1:per + 2]) * state + piece[0:per]
    loop(1, np_, lambda k: p2(k).start())
    p2_own = pltpu.make_async_copy(eb.at[g_me], me.at[g_me], loc_s.at[6])
    p2_own.start()

    wrelay(1).wait_recv()
    wrelay(1).start()
    def p2_arrival(k):
        o = lax.rem(g_me + k, np_)
        rc(eb.at[o], me.at[o], p2_s.at[k], p2_r.at[o], dev(z, x, y, other)).wait_recv()

    p2_own.wait()
    loop(1, np_, p2_arrival)
    entry = me[...].astype(F32).reshape(2, SEG, DH)

    def unit(m):
        return (m * lax.rsqrt(jnp.mean(m * m, axis=1, keepdims=True) + 1e-06)).astype(BF16)

    for j in range(2):
        if j == 0:
            mem = (entry[0], entry[1])
        else:
            mem = tuple(decays[0] * entry[u] + written[0][u] for u in range(2))
        mk, mv = unit(mem[0]), unit(mem[1])
        s = lax.dot_general(queries[j], mk, nt, preferred_element_type=F32) * factor
        w = jax.nn.sigmoid(s - bias).astype(BF16)
        a = jnp.dot(w, mv, preferred_element_type=F32) + token_part[j]
        satt[j] = jnp.where(sub < lens[j], a, 0.0).astype(BF16)

    def att_slot(cc):
        return ratt.at[:, columns(jnp.where(hx == cc, 0, 2) + px)]

    def att_copy(j, cc):
        return rc(satt.at[j], att_slot(cc), at_s.at[j, cc], at_r.at[x],
                  dev(z, 2 * c + j, y, cc))

    for j in range(2):
        for cc in range(NC):
            mine = jnp.logical_and(x == 2 * c + j, c == cc)

            @pl.when(jnp.logical_not(mine))
            def _():
                att_copy(j, cc).start()

            @pl.when(mine)
            def _():
                pltpu.make_async_copy(satt.at[j], att_slot(cc), at_r.at[x]).start()

    for p in (0, 1):
        late_col = xr if p == 0 else xl
        for col in (late_col, xm):
            rc(wf.at[p, col], wf.at[p, col], wf_s.at[0], wx_r.at[p, col],
               dev(z, xr, y, c)).wait_recv()
        wx_own[p].wait()
    for xx in range(NX):
        rc(satt.at[0], ratt.at[:, 0:128], at_s.at[0, 0], at_r.at[xx],
           dev(z, x, y, other)).wait_recv()

    att0, att1 = ratt[:, 0:256], ratt[:, 256:512]

    def product(yy):
        total = jnp.zeros((SEG, 2 * NX * ROWS), F32)
        for p, a in ((0, att0), (1, att1)):
            w = jnp.concatenate(
                [wf[p, xx, yy, u] for u in range(2) for xx in range(NX)], axis=0
            )
            total = total + lax.dot_general(a, w, nt, preferred_element_type=F32)
        return total

    def pb(i):
        return rc(sb.at[ys[i]], orx.at[y], pb_s.at[ys[i]], pb_r.at[y], dev(z, x, ys[i], c))

    for i in ([2] if ny > 2 else []) + [i for i in range(1, ny) if i != 2]:
        sb[ys[i]] = product(ys[i]).astype(BF16)
        pb(i).start()
    result = product(y)
    for i in range(1, ny):
        rc(sb.at[ys[i]], orx.at[ys[i]], pb_s.at[ys[i]], pb_r.at[ys[i]],
           dev(z, x, ys[i], c)).wait_recv()
        result = result + orx[ys[i]].astype(F32)
    out[...] = result.astype(BF16)

    for a in range(4):
        ring_drain(a)
    mqc.wait_send()
    swap.wait_send()
    for i in range(1, NX):
        t1(i).wait_send()
    for i in range(1, ny):
        t2(i, h_me).wait_send()
    for i in range(ny):
        t3(ys[i] * NC + c).wait_send()
    for way in (0, 1):
        for p in (0, 1):
            wx(way, p).wait_send()
        wrelay(way).wait_send()
    for i in range(2):
        for cc in range(NC):
            mine = jnp.logical_and(x == 2 * c + i, c == cc)

            @pl.when(jnp.logical_not(mine))
            def _():
                for n in range(3):
                    reduce_copy(i, cc, n).wait_send()
    loop(1, np_, lambda k: p1(k).wait_send())
    loop(1, np_, lambda k: p2(k).wait_send())
    for j in range(2):
        for cc in range(NC):
            mine = jnp.logical_and(x == 2 * c + j, c == cc)

            @pl.when(jnp.logical_not(mine))
            def _():
                att_copy(j, cc).wait_send()
    for i in range(1, ny):
        pb(i).wait_send()


def solution(mesh):
    nz = mesh.shape["seq"] // NX
    ny = mesh.shape["head"] // NC

    def body(tokens, gain, w_query, w_key, w_value, w_out, mem_query, score_scale, decay, seg_len):
        vm = pl.BlockSpec(memory_space=pltpu.VMEM)
        np_ = nz * NC
        per = 2 * SEG // np_
        dma = pltpu.SemaphoreType.DMA
        width = tokens.shape[1]
        scratch = [
            pltpu.VMEM(tokens.shape, BF16),
            pltpu.VMEM((gain.shape[0] // 128, 128), F32),
            pltpu.VMEM((128, 256), BF16),
            pltpu.SMEM((1, 2), F32),
            pltpu.SMEM((1, 2), F32),
            pltpu.SMEM((1,), jnp.int32),
            pltpu.VMEM((nz, ROWS, 256), BF16),
            pltpu.VMEM((nz, ROWS, 256), BF16),
            pltpu.VMEM((nz, ROWS, 256), BF16),
            pltpu.VMEM((ny, NC, 2, ROWS, 256), BF16),
            pltpu.VMEM((ny, 2, ROWS, 256), BF16),
            pltpu.VMEM((2, NX, ny, 2, ROWS, 256), BF16),
            pltpu.VMEM((2, 128, 256), BF16),
            pltpu.VMEM((NX, 128, 128), BF16),
            pltpu.VMEM((NX * SEG, nz * ROWS), BF16),
            pltpu.VMEM((NX * SEG, nz * ROWS), BF16),
            pltpu.VMEM((2, NC, 256, 256), BF16),
            pltpu.VMEM((NX, 256, 256), BF16),
            pltpu.VMEM((2, NC, 256, 128), BF16),
            pltpu.VMEM((NX, 256, 128), BF16),
            pltpu.VMEM((2, NC, 16, 256), F32),
            pltpu.VMEM((NX, 16, 256), F32),
            pltpu.VMEM((np_, per + 8, 128), BF16),
            pltpu.VMEM((np_, per + 8, 128), BF16),
            pltpu.VMEM((np_, per, 128), BF16),
            pltpu.VMEM((np_, per, 128), BF16),
            pltpu.VMEM((2, 128, 128), BF16),
            pltpu.VMEM((128, 512), BF16),
            pltpu.VMEM((ny, 128, width), BF16),
            pltpu.VMEM((ny, 128, width), BF16),
            dma((4, 2, nz // 2 + 2)), dma((4, nz)), dma((9,)), dma, dma,
            dma((NX,)), dma((NX,)), dma((ny,)), dma((ny,)), dma((ny,)), dma((ny,)),
            dma((2, 2)), dma((NX,)), dma((2, 2)), dma((NX,)), dma((2, 2)), dma((NX,)),
            dma, dma, dma((2, 2)), dma((2, NX)), dma((2,)),
            dma((np_,)), dma((np_,)), dma((np_,)), dma((np_,)),
            dma((2, 2)), dma((NX,)), dma((ny,)), dma((ny,)), dma((6,)),
        ]
        return pl.pallas_call(
            functools.partial(kernel, nz, ny),
            out_shape=jax.ShapeDtypeStruct(tokens.shape, BF16),
            in_specs=[pl.BlockSpec(memory_space=pl.ANY)] * 10,
            out_specs=vm,
            scratch_shapes=scratch,
            compiler_params=pltpu.CompilerParams(
                collective_id=0, has_side_effects=True, vmem_limit_bytes=60 * 1024 * 1024
            ),
        )(
            tokens, gain.reshape(-1, 128), w_query, w_key, w_value, w_out.T, mem_query,
            score_scale.reshape(1, 2), decay, seg_len,
        )

    return jax.shard_map(
        body,
        mesh=mesh,
        in_specs=(
            P("seq", "head"), P(None), P("seq", "head"), P("seq", "head"), P("seq", "head"),
            P("head", "seq"), P(None, "head"), P("head"), P("seq", "head"), P("seq"),
        ),
        out_specs=P("seq", "head"),
        check_vma=False,
    )
```

```python
import functools
import math

import jax
import jax.numpy as jnp
from jax import lax
from jax.experimental import pallas as pl
from jax.experimental.pallas import tpu as pltpu
from jax.sharding import PartitionSpec as P

MESH = pl.DeviceIdType.MESH
NX = 4
NC = 2
SEG = 128
DH = 128
ROWS = 64
F32 = jnp.float32
BF16 = jnp.bfloat16


def kernel(
    nz, ny,
    tok_h, gain_h, wq, wk, wv, wo, mq_h, scale_h, decay_h, seglen_h,
    out,
    tok, gain, mq, scale, decay, seglen,
    wqb, wkb, wvb, wr, wf, mqb, tsend, tkb, tgb,
    skv, rkv, sq, rq, sside, rside,
    dv, db, tb, rb, eb, me, satt, ratt, sb, orx,
    ring_s, ring_r, loc_s, mq_s, mq_r, t1_s, t1_r, t2_s, t2_r, t3_s, t3_r,
    kv_s, kv_r, q_s, q_r, sd_s, sd_r, wx_s, wx_r,
    p0_s, p0_r, p1_s, p1_r, p2_s, p2_r, at_s, at_r, pb_s, pb_r, in_s,
):
    seq = lax.axis_index("seq")
    head = lax.axis_index("head")
    z, x = lax.div(seq, NX), lax.rem(seq, NX)
    y, c = lax.div(head, NC), lax.rem(head, NC)
    other = 1 - c
    hx, px = lax.div(x, 2), lax.rem(x, 2)
    features = nz * NX * ROWS

    def dev(zz, xx, yy, cc):
        return {"seq": zz * NX + xx, "head": yy * NC + cc}

    def rc(src, dst, ssem, rsem, target):
        return pltpu.make_async_remote_copy(
            src_ref=src, dst_ref=dst, send_sem=ssem, recv_sem=rsem,
            device_id=target, device_id_type=MESH,
        )

    def loop(lo_, hi_, f):
        def body(k, carry):
            f(k)
            return carry
        lax.fori_loop(lo_, hi_, body, 0)

    zr, zl = lax.rem(z + 1, nz), lax.rem(z + nz - 1, nz)
    xs = [lax.rem(x + i, NX) for i in range(NX)]
    ys = [lax.rem(y + i, ny) for i in range(ny)]

    stage = [
        pltpu.make_async_copy(a, b, in_s.at[n])
        for n, (a, b) in enumerate((
            (tok_h, tok), (gain_h, gain), (mq_h, mq), (scale_h, scale), (decay_h, decay),
            (seglen_h, seglen),
        ))
    ]
    for cp in stage:
        cp.start()

    barrier = pltpu.get_barrier_semaphore()
    near = [dev(zr, x, y, c), dev(zl, x, y, c), dev(z, x, y, other)]
    near += [dev(z, xx, y, cc) for xx in xs[1:] for cc in range(NC)]
    near += [dev(z, x, yy, c) for yy in ys[1:]]
    for d in near:
        pl.semaphore_signal(barrier, inc=1, device_id=d, device_id_type=MESH)
    pl.semaphore_wait(barrier, len(near))

    srcs = (wk, wv, wo, wq)

    def slot(a, b):
        if a == 2:
            return wr.at[lax.div(b, 2 * NC), lax.rem(lax.div(b, 2), NC), lax.rem(b, 2)]
        return (wkb, wvb, None, wqb)[a].at[b]

    def block(way, t):
        return lax.rem(z + nz - (t - 1), nz) if way == 0 else lax.rem(z + t - 1, nz)

    def ring(a, way, t):
        b = block(way, t)
        return rc(srcs[a] if t == 1 else slot(a, b), slot(a, b),
                  ring_s.at[a, way, t], ring_r.at[a, b], dev(zr if way == 0 else zl, x, y, c))

    def spread(b, i, src):
        to = lax.rem(lax.div(b, 2), NC)
        yy, u = lax.div(b, 2 * NC), lax.rem(b, 2)
        r = jnp.where(to == c, 0, 1)
        target = dev(z, x, y, other) if i == 0 else dev(z, xs[i], y, to)
        return rc(src, wf.at[r, x, yy, u], wx_s.at[b, i], wx_r.at[r, x, yy * 2 + u], target)

    def spread_start(b, src):
        for i in range(1, NX):
            spread(b, i, src).start()
        yy, u = lax.div(b, 2 * NC), lax.rem(b, 2)
        mine = lax.rem(lax.div(b, 2), NC) == c

        @pl.when(jnp.logical_not(mine))
        def _():
            spread(b, 0, src).start()

        @pl.when(mine)
        def _():
            pltpu.make_async_copy(src, wf.at[0, x, yy, u], wx_r.at[0, x, yy * 2 + u]).start()

    def spread_drain(b):
        src = slot(2, b)
        for i in range(1, NX):
            spread(b, i, src).wait_send()

        @pl.when(lax.rem(lax.div(b, 2), NC) != c)
        def _():
            spread(b, 0, src).wait_send()

    def spread_arrived(n):
        r, xx, v = lax.div(n, NX * ny * 2), lax.rem(lax.div(n, ny * 2), NX), lax.rem(n, ny * 2)
        ref = wf.at[r, xx, lax.div(v, 2), lax.rem(v, 2)]
        rc(ref, ref, wx_s.at[0, 0], wx_r.at[r, xx, v], dev(z, x, y, other)).wait_recv()

    half = nz // 2

    def long_way(a):
        return a % 2

    def ring_first(a):
        for way in (0, 1):
            ring(a, way, 1).start()

    def ring_mid(arrays, t):
        for a in arrays:
            for way in (0, 1):
                cp = ring(a, way, t)
                cp.wait_recv()
                cp.start()
                if a == 2:
                    spread_start(block(way, t), slot(2, block(way, t)))

    def ring_last(arrays):
        for a in arrays:
            for way in (0, 1):
                cp = ring(a, way, half)
                cp.wait_recv()
                if way == long_way(a):
                    cp.start()
                if a == 2:
                    spread_start(block(way, half), slot(2, block(way, half)))
        for a in arrays:
            way = long_way(a)
            ring(a, way, half + 1).wait_recv()
            if a == 2:
                spread_start(block(way, half + 1), slot(2, block(way, half + 1)))

    def ring_drain(a):
        for way in (0, 1):
            for t in range(1, half + (1 if way == long_way(a) else 0)):
                ring(a, way, t).wait_send()

    early = (0, 1, 3, 2)
    for a in early:
        ring_first(a)

    spread_start(z, srcs[2])
    own = [pltpu.make_async_copy(srcs[a], slot(a, z), loc_s.at[a]) for a in (0, 1, 3)]
    for cp in own:
        cp.start()

    stage[0].wait()
    for i in range(NX):
        tsend[i] = jnp.concatenate(
            [tok[:, 64 * i:64 * i + 64], tok[:, 256 + 64 * i:256 + 64 * i + 64]], axis=1
        )

    def columns(h):
        return pl.ds(pl.multiple_of(h * 128, 128), 128)

    def rows(i):
        return pl.ds(pl.multiple_of(i * 128, 128), 128)

    h_me = y * NC + c

    def t1(i):
        xx = xs[i]
        return rc(tsend.at[xx], tkb.at[rows(x), columns(h_me)], t1_s.at[xx], t1_r.at[x],
                  dev(z, xx, y, c))

    for i in range(1, NX):
        t1(i).start()
    t1_own = pltpu.make_async_copy(tsend.at[x], tkb.at[rows(x), columns(h_me)], loc_s.at[4])
    t1_own.start()

    stage[2].wait()
    mqc = rc(mq, mqb.at[c], mq_s, mq_r, dev(z, x, y, other))
    mqc.start()

    steps = list(range(2, half)) + [half]

    def advance(n):
        for t in steps[:n]:
            if t < half:
                ring_mid(early, t)
            else:
                ring_last(early)
        del steps[:n]

    advance(1)
    t1_own.wait()
    for i in range(1, NX):
        xx = xs[i]
        rc(tsend.at[xx], tkb.at[rows(xx), columns(h_me)], t1_s.at[xx], t1_r.at[xx],
           dev(z, xx, y, c)).wait_recv()

    def t2(i, hh):
        return rc(tkb.at[:, columns(hh)], tkb.at[:, columns(hh)], t2_s.at[i],
                  t2_r.at[lax.div(hh, NC)], dev(z, x, ys[i], c))

    def t3(hh):
        yy = lax.div(hh, NC)
        return rc(tkb.at[:, columns(hh)], tkb.at[:, columns(hh)], t3_s.at[yy], t3_r.at[yy],
                  dev(z, x, y, other))

    for i in range(1, ny):
        t2(i, h_me).start()
    t3(h_me).start()
    advance(2)
    for i in range(1, ny):
        hh = ys[i] * NC + c
        t2(i, hh).wait_recv()
        t3(hh).start()
    stage[1].wait()
    ga = gain[pl.ds(hx, ny * NC, stride=4), :]
    gb = gain[pl.ds(2 + hx, ny * NC, stride=4), :]
    even = jnp.concatenate([ga[:, :64], gb[:, :64]], axis=1)
    odd = jnp.concatenate([ga[:, 64:], gb[:, 64:]], axis=1)
    g = jnp.where(px == 0, even, odd)
    ones = jnp.ones((8, 128), BF16)

    def stats(h, ss):
        t = tkb[:, h * 128:h * 128 + 128].astype(F32)
        tgb[:, h * 128:h * 128 + 128] = (t * g[h:h + 1, :]).astype(BF16)
        return ss + lax.dot_general(ones, (t * t).astype(BF16), (((1,), (1,)), ((), ())),
                                    preferred_element_type=F32)

    advance(2)
    for i in range(ny):
        hh = ys[i] * NC + other
        rc(tkb.at[:, columns(hh)], tkb.at[:, columns(hh)], t3_s.at[ys[i]], t3_r.at[ys[i]],
           dev(z, x, y, other)).wait_recv()
    ss = jnp.zeros((8, NX * SEG), F32)
    for h in range(ny):
        ss = stats(h, ss)
    advance(1)
    for h in range(ny, ny * NC):
        ss = stats(h, ss)
    advance(len(steps))
    for cp in own:
        cp.wait()

    depth = nz * ROWS
    def project(a, buf):
        part = jnp.dot(tgb[...], buf[...].reshape(depth, 2 * DH), preferred_element_type=F32)
        part = part.astype(BF16)
        for i in range(2):
            for cc in range(NC):
                block = part[cc * 256:cc * 256 + 256, i * DH:i * DH + DH]
                if a < 2:
                    skv[i, cc, :, a * DH:a * DH + DH] = block
                else:
                    sq[i, cc] = block

    for cp in stage[3:]:
        cp.wait()
    row_id = lax.broadcasted_iota(jnp.int32, (8, 256), 0)
    length = seglen[0].astype(F32)
    for i in range(2):
        facts = jnp.where(row_id == 0, decay[0, i], jnp.where(row_id == 1, scale[0, i], length))
        for cc in range(NC):
            sside[i, cc, 0:8] = ss[:, cc * 256:cc * 256 + 256]
            sside[i, cc, 8:16] = facts

    trio = ((sside, rside, sd_s, sd_r), (skv, rkv, kv_s, kv_r), (sq, rq, q_s, q_r))

    def reduce_copy(i, cc, n):
        xx = 2 * c + i
        target = dev(z, xx, y, cc)
        src, dst, ssem, rsem = trio[n]
        return rc(src.at[i, cc], dst.at[x], ssem.at[i, cc], rsem.at[x], target)

    def local_copy(i, cc, n):
        src, dst, ssem, rsem = trio[n]
        return pltpu.make_async_copy(src.at[i, cc], dst.at[x], rsem.at[x])

    def reduce_start(n):
        for i in range(2):
            for cc in range(NC):
                mine = jnp.logical_and(x == 2 * c + i, c == cc)

                @pl.when(jnp.logical_not(mine))
                def _():
                    reduce_copy(i, cc, n).start()

                @pl.when(mine)
                def _():
                    local_copy(i, cc, n).start()

    reduce_start(0)
    project(0, wkb)
    project(1, wvb)
    reduce_start(1)
    project(2, wqb)
    reduce_start(2)

    def reduce_wait(n, xx):
        target = dev(z, x, y, other)
        src, dst, ssem, rsem = trio[n]
        rc(src.at[0, 0], dst.at[xx], ssem.at[0, 0], rsem.at[xx], target).wait_recv()

    for xx in range(NX):
        reduce_wait(0, xx)

    np_ = nz * NC
    g_me = z * NC + c

    def owner(k):
        o = lax.rem(g_me + k, np_)
        return o, dev(lax.div(o, NC), x, y, lax.rem(o, NC))

    def p0(k):
        return rc(dv, db.at[g_me], p0_s.at[k], p0_r.at[g_me], owner(k)[1])

    both = rside[2 * c, 8:16][0:1, 0:128] * rside[2 * c + 1, 8:16][0:1, 0:128]
    dv[...] = jnp.broadcast_to(both, (8, 128))
    loop(1, np_, lambda k: p0(k).start())
    p0_own = pltpu.make_async_copy(dv, db.at[g_me], loc_s.at[4])
    p0_own.start()
    for xx in range(NX):
        reduce_wait(1, xx)
    total = rside[0, 0:8]
    for xx in range(1, NX):
        total = total + rside[xx, 0:8]
    r8 = lax.rsqrt(total * (1.0 / features) + 1e-05)
    kv = rkv[0].astype(F32)
    for xx in range(1, NX):
        kv = kv + rkv[xx].astype(F32)

    rt, keys, values, lens, decays = [], [], [], [], []
    for j in range(2):
        wide = jnp.broadcast_to(r8[0:1, j * 128:j * 128 + 128], (128, 128)).T
        rt.append(wide)
        part = kv[j * 128:j * 128 + 128]
        keys.append((part[:, :DH] * wide).astype(BF16))
        values.append((part[:, DH:] * wide).astype(BF16))
        facts = rside[2 * c + j, 8:16]
        decays.append(facts[0:1, 0:128])
        lens.append(facts[2:3, 0:128])
    score_scale = rside[x, 8:16][1:2, 0:128]

    inverse_root = 1.0 / math.sqrt(DH)
    rc(mq, mqb.at[other], mq_s, mq_r, dev(z, x, y, other)).wait_recv()
    mq_own = mq[:, pl.ds(pl.multiple_of(px * 128, 128), 128)]
    mq_other = mqb[other][:, :].astype(F32)
    mq_other = jnp.where(px == 0, mq_other[:, :DH], mq_other[:, DH:]).astype(BF16)
    mqh = jnp.where(hx == c, mq_own.astype(F32), mq_other.astype(F32)).astype(BF16)

    lane = lax.broadcasted_iota(jnp.int32, (SEG, SEG), 1).astype(F32)
    sub = lax.broadcasted_iota(jnp.int32, (SEG, SEG), 0).astype(F32)
    nt = (((1,), (1,)), ((), ()))
    written = []
    for j in range(2):
        s = lax.dot_general(mqh, keys[j], nt, preferred_element_type=F32) * inverse_root
        w = jax.nn.sigmoid(s - math.log(SEG))
        w = jnp.where(lane < lens[j], w, 0.0).astype(BF16)
        written.append((
            jnp.dot(w, keys[j], preferred_element_type=F32),
            jnp.dot(w, values[j], preferred_element_type=F32),
        ))

    per = 2 * SEG // np_
    for u in range(2):
        t = decays[1] * written[0][u] + written[1][u]
        tb[u * (np_ // 2):(u + 1) * (np_ // 2)] = t.reshape(np_ // 2, per, 128).astype(BF16)

    def p1(k):
        o, target = owner(k)
        return rc(tb.at[o], rb.at[g_me], p1_s.at[k], p1_r.at[g_me], target)

    def p2(k):
        o, target = owner(k)
        return rc(eb.at[o], me.at[g_me], p2_s.at[k], p2_r.at[g_me], target)

    loop(1, np_, lambda k: p1(k).start())
    p1_own = pltpu.make_async_copy(tb.at[g_me], rb.at[g_me], loc_s.at[5])
    p1_own.start()

    for xx in range(NX):
        reduce_wait(2, xx)
    qs = rq[0].astype(F32)
    for xx in range(1, NX):
        qs = qs + rq[xx].astype(F32)
    bias = math.log(SEG + SEG)
    factor = score_scale * inverse_root
    queries, token_part = [], []
    for j in range(2):
        q = (qs[j * 128:j * 128 + 128] * rt[j]).astype(BF16)
        queries.append(q)
        s = lax.dot_general(q, keys[j], nt, preferred_element_type=F32) * factor
        w = jax.nn.sigmoid(s - bias)
        keep = jnp.logical_and(lane <= sub, lane < lens[j])
        w = jnp.where(keep, w, 0.0).astype(BF16)
        token_part.append(jnp.dot(w, values[j], preferred_element_type=F32))

    def p1_arrival(k):
        o = lax.rem(g_me + k, np_)
        rc(tb.at[o], rb.at[o], p1_s.at[k], p1_r.at[o], dev(z, x, y, other)).wait_recv()

    def p0_arrival(k):
        o = owner(k)[0]
        rc(dv, db.at[o], p0_s.at[k], p0_r.at[o], dev(z, x, y, other)).wait_recv()

    p0_own.wait()
    loop(1, np_, p0_arrival)
    p1_own.wait()
    loop(1, np_, p1_arrival)
    state = jnp.zeros((per, 128), F32)
    for k in range(np_):
        eb[k] = state.astype(BF16)
        state = db[k][0:1] * state + rb[k].astype(F32)
    loop(1, np_, lambda k: p2(k).start())
    p2_own = pltpu.make_async_copy(eb.at[g_me], me.at[g_me], loc_s.at[6])
    p2_own.start()

    def p2_arrival(k):
        o = lax.rem(g_me + k, np_)
        rc(eb.at[o], me.at[o], p2_s.at[k], p2_r.at[o], dev(z, x, y, other)).wait_recv()

    for a in range(4):
        ring_drain(a)
    mqc.wait_send()
    for i in range(1, NX):
        t1(i).wait_send()
    for i in range(1, ny):
        t2(i, h_me).wait_send()
    for i in range(ny):
        t3(ys[i] * NC + c).wait_send()
    loop(0, nz, spread_drain)
    for i in range(2):
        for cc in range(NC):
            mine = jnp.logical_and(x == 2 * c + i, c == cc)

            @pl.when(jnp.logical_not(mine))
            def _():
                for n in range(3):
                    reduce_copy(i, cc, n).wait_send()
    loop(1, np_, lambda k: p0(k).wait_send())
    loop(1, np_, lambda k: p1(k).wait_send())
    p2_own.wait()
    loop(1, np_, p2_arrival)
    entry = me[...].astype(F32).reshape(2, SEG, DH)

    def unit(m):
        return (m * lax.rsqrt(jnp.mean(m * m, axis=1, keepdims=True) + 1e-06)).astype(BF16)

    for j in range(2):
        if j == 0:
            mem = (entry[0], entry[1])
        else:
            mem = tuple(decays[0] * entry[u] + written[0][u] for u in range(2))
        mk, mv = unit(mem[0]), unit(mem[1])
        s = lax.dot_general(queries[j], mk, nt, preferred_element_type=F32) * factor
        w = jax.nn.sigmoid(s - bias).astype(BF16)
        a = jnp.dot(w, mv, preferred_element_type=F32) + token_part[j]
        satt[j] = jnp.where(sub < lens[j], a, 0.0).astype(BF16)

    def att_slot(cc):
        return ratt.at[:, columns(jnp.where(hx == cc, 0, 2) + px)]

    def att_copy(j, cc):
        return rc(satt.at[j], att_slot(cc), at_s.at[j, cc], at_r.at[x],
                  dev(z, 2 * c + j, y, cc))

    for j in range(2):
        for cc in range(NC):
            mine = jnp.logical_and(x == 2 * c + j, c == cc)

            @pl.when(jnp.logical_not(mine))
            def _():
                att_copy(j, cc).start()

            @pl.when(mine)
            def _():
                pltpu.make_async_copy(satt.at[j], att_slot(cc), at_r.at[x]).start()

    for xx in range(NX):
        rc(satt.at[0], ratt.at[:, 0:128], at_s.at[0, 0], at_r.at[xx],
           dev(z, x, y, other)).wait_recv()

    loop(0, 2 * NX * ny * 2, spread_arrived)

    att0, att1 = ratt[:, 0:256], ratt[:, 256:512]

    def product(yy):
        total = jnp.zeros((SEG, 2 * NX * ROWS), F32)
        for p, a in ((0, att0), (1, att1)):
            w = jnp.concatenate(
                [wf[p, xx, yy, u] for u in range(2) for xx in range(NX)], axis=0
            )
            total = total + lax.dot_general(a, w, nt, preferred_element_type=F32)
        return total

    def pb(i):
        return rc(sb.at[ys[i]], orx.at[y], pb_s.at[ys[i]], pb_r.at[y], dev(z, x, ys[i], c))

    for i in ([2] if ny > 2 else []) + [i for i in range(1, ny) if i != 2]:
        sb[ys[i]] = product(ys[i]).astype(BF16)
        pb(i).start()
    result = product(y)
    for i in range(1, ny):
        rc(sb.at[ys[i]], orx.at[ys[i]], pb_s.at[ys[i]], pb_r.at[ys[i]],
           dev(z, x, ys[i], c)).wait_recv()
        result = result + orx[ys[i]].astype(F32)
    out[...] = result.astype(BF16)

    loop(1, np_, lambda k: p2(k).wait_send())
    for j in range(2):
        for cc in range(NC):
            mine = jnp.logical_and(x == 2 * c + j, c == cc)

            @pl.when(jnp.logical_not(mine))
            def _():
                att_copy(j, cc).wait_send()
    for i in range(1, ny):
        pb(i).wait_send()


def solution(mesh):
    nz = mesh.shape["seq"] // NX
    ny = mesh.shape["head"] // NC

    def body(tokens, gain, w_query, w_key, w_value, w_out, mem_query, score_scale, decay, seg_len):
        vm = pl.BlockSpec(memory_space=pltpu.VMEM)
        np_ = nz * NC
        per = 2 * SEG // np_
        dma = pltpu.SemaphoreType.DMA
        width = tokens.shape[1]
        scratch = [
            pltpu.VMEM(tokens.shape, BF16),
            pltpu.VMEM((gain.shape[0] // 128, 128), F32),
            pltpu.VMEM((128, 256), BF16),
            pltpu.SMEM((1, 2), F32),
            pltpu.SMEM((1, 2), F32),
            pltpu.SMEM((1,), jnp.int32),
            pltpu.VMEM((nz, ROWS, 256), BF16),
            pltpu.VMEM((nz, ROWS, 256), BF16),
            pltpu.VMEM((nz, ROWS, 256), BF16),
            pltpu.VMEM((ny, NC, 2, ROWS, 256), BF16),
            pltpu.VMEM((2, NX, ny, 2, ROWS, 256), BF16),
            pltpu.VMEM((2, 128, 256), BF16),
            pltpu.VMEM((NX, 128, 128), BF16),
            pltpu.VMEM((NX * SEG, nz * ROWS), BF16),
            pltpu.VMEM((NX * SEG, nz * ROWS), BF16),
            pltpu.VMEM((2, NC, 256, 256), BF16),
            pltpu.VMEM((NX, 256, 256), BF16),
            pltpu.VMEM((2, NC, 256, 128), BF16),
            pltpu.VMEM((NX, 256, 128), BF16),
            pltpu.VMEM((2, NC, 16, 256), F32),
            pltpu.VMEM((NX, 16, 256), F32),
            pltpu.VMEM((8, 128), F32),
            pltpu.VMEM((np_, 8, 128), F32),
            pltpu.VMEM((np_, per, 128), BF16),
            pltpu.VMEM((np_, per, 128), BF16),
            pltpu.VMEM((np_, per, 128), BF16),
            pltpu.VMEM((np_, per, 128), BF16),
            pltpu.VMEM((2, 128, 128), BF16),
            pltpu.VMEM((128, 512), BF16),
            pltpu.VMEM((ny, 128, width), BF16),
            pltpu.VMEM((ny, 128, width), BF16),
            dma((4, 2, nz // 2 + 2)), dma((4, nz)), dma((9,)), dma, dma,
            dma((NX,)), dma((NX,)), dma((ny,)), dma((ny,)), dma((ny,)), dma((ny,)),
            dma((2, 2)), dma((NX,)), dma((2, 2)), dma((NX,)), dma((2, 2)), dma((NX,)),
            dma((nz, NX)), dma((2, NX, ny * 2)),
            dma((np_,)), dma((np_,)), dma((np_,)), dma((np_,)), dma((np_,)), dma((np_,)),
            dma((2, 2)), dma((NX,)), dma((ny,)), dma((ny,)), dma((6,)),
        ]
        return pl.pallas_call(
            functools.partial(kernel, nz, ny),
            out_shape=jax.ShapeDtypeStruct(tokens.shape, BF16),
            in_specs=[pl.BlockSpec(memory_space=pl.ANY)] * 10,
            out_specs=vm,
            scratch_shapes=scratch,
            compiler_params=pltpu.CompilerParams(
                collective_id=0, has_side_effects=True, vmem_limit_bytes=60 * 1024 * 1024
            ),
        )(
            tokens, gain.reshape(-1, 128), w_query, w_key, w_value, w_out.T, mem_query,
            score_scale.reshape(1, 2), decay, seg_len,
        )

    return jax.shard_map(
        body,
        mesh=mesh,
        in_specs=(
            P("seq", "head"), P(None), P("seq", "head"), P("seq", "head"), P("seq", "head"),
            P("head", "seq"), P(None, "head"), P("head"), P("seq", "head"), P("seq"),
        ),
        out_specs=P("seq", "head"),
        check_vma=False,
    )
```
